128 devices in a mesh: segment: 4 (over z), exp: 32 (over y, x, core).
Axes of the slice: x: 4, y: 4, z: 4, core: 2. Of those that a mesh axis runs over, the one named last changes fastest.
Arguments:
- hidden_rows: bfloat16 [16384, 2048], P(('segment', 'exp')), may hold values from -60 to 60, as said below
- norm_gain: float32 [2048], replicated, may hold values from 0.5 to 1.5
- router_weight: bfloat16 [2048, 64], replicated, may hold values from -0.25 to 0.25
- expert_ids: int32 [16384, 6], P(('segment', 'exp')), may hold values from 0 to 63, all different within a row; in each aligned block of 64 rows (0 to 63, 64 to 127, ...) at most 7 rows name the same one
- gate_weight: bfloat16 [4, 32, 704, 2048], P('segment', 'exp'), may hold values from -0.125 to 0.125
- up_weight: bfloat16 [4, 32, 704, 2048], P('segment', 'exp'), may hold values from -0.125 to 0.125
- down_weight: bfloat16 [4, 32, 704, 2048], P('segment', 'exp'), may hold values from -0.15625 to 0.15625
- latent_gain: float32 [2048], replicated, may hold values from 0.5 to 1.5
- kv_weight: bfloat16 [2048, 512], replicated, may hold values from -0.125 to 0.125
Outputs:
- expert_mix: bfloat16 [16384, 2048], P(('segment', 'exp'))
- latents: bfloat16 [16384, 512], P(('segment', 'exp'))
- gram_input: float32 [4, 32, 1024, 2048], P('segment', 'exp')
- gram_hidden: float32 [4, 32, 704, 1408], P('segment', 'exp')
The draws below stay inside these ranges and needn't reach their ends.
Inputs may be any that keep to these rules, and one draw needn't show every extreme that they name: `expert_ids`: each row names 6 different experts and every expert is named somewhere. In each aligned block of 64 rows (one micro-batch of one device) no expert is named more than 7 times, and in some blocks some expert is named exactly 7 times. `hidden_rows`: activations of the attention section.
All inputs are finite; a program needn't handle non-finite values.
Results may differ from the reference program's by a relative error of at most 0.0068.
Values may be sent and summed in bfloat16 or wider, within the bound.
No kernel may reach another device: no remote copies, remote signals or barrier semaphores. Data moves between devices by JAX's collectives and lax.ppermute only.
A program may use at most 192 MiB of HBM per device.

```python
import math
import jax
import jax.numpy as jnp
import numpy as np
from jax import lax

D = 2048
FF = 1408
KV_RANK = 512
TOPK = 6
MB_TOK = 64
TOKENS = 16384
PAIRS = 2
EXPERTS = 64
HALF = 704
CAP = 7
N_SEGMENT = 4
N_EXP = 32


def draw_hidden_rows(key, part):
    key_base, key_rows, key_cols = jax.random.split(key, 3)
    row_scale = jnp.exp(jax.random.uniform(key_rows, (TOKENS, 1), jnp.float32, math.log(0.3), math.log(3.0)))
    col_scale = jnp.exp(jax.random.uniform(key_cols, (1, D), jnp.float32, math.log(0.4), math.log(4.0)))
    values = jnp.clip(jax.random.normal(key_base, (TOKENS, D), jnp.float32), -5.0, 5.0)
    return (values * row_scale * col_scale).astype(jnp.bfloat16)


def steps_of(own_key, shape, cuts, low, high):
    def one(axis_at, blocks):
        draws = jax.random.uniform(jax.random.fold_in(jax.random.fold_in(own_key, 6), axis_at), (blocks,), jnp.float32, low / len(cuts), high / len(cuts))
        return jnp.repeat(jnp.exp(draws), shape[axis_at] // blocks).reshape((-1,) + (1,) * (len(shape) - axis_at - 1))

    factor_of = one(*cuts[0])
    for cut in cuts[1:]:
        factor_of = factor_of * one(*cut)
    return factor_of


def shared_out(own_key, own, number, rows, number_of, top, limit, lean):
    ranking = jax.random.permutation(own_key, number_of)
    crowded, common = load_shares(number_of, rows * top, limit, lean, True), load_shares(number_of, rows * top, limit, lean, False)
    places = jnp.arange(number_of)

    def named(sizes, offset_by):
        used = int((sizes > 0).sum())
        fixed = max(1, used // 4)
        passed = fixed + (places - fixed + offset_by * (used - fixed)) % max(1, number_of - fixed)
        return jnp.zeros((number_of,), jnp.int32).at[ranking[jnp.where(places < fixed, places, passed)]].set(jnp.asarray(sizes, jnp.int32))

    sizes = jnp.where(number % 4 == 0, named(crowded, number // 4), named(common, number - number // 4 - 1))
    mixed = jax.random.permutation(jax.random.fold_in(own, 3), number_of)
    donor, sink = mixed[0:number_of // 2 * 2:2], mixed[1:number_of // 2 * 2:2]
    margin = jnp.minimum(sizes[donor] - 1, limit - sizes[sink]) // 2
    margin = jnp.where((donor == ranking[0]) | (sink == ranking[0]) | (sizes[sink] == 0), 0, jnp.maximum(margin, 0))
    passed = jax.random.randint(jax.random.fold_in(own, 4), (number_of // 2,), 0, 1 << 20) % (margin + 1)
    sizes = sizes.at[donor].add(-passed).at[sink].add(passed)
    members = jnp.searchsorted(jnp.cumsum(sizes), jnp.arange(rows * top), side="right").astype(jnp.int32)
    table = members.reshape(top, rows).T
    table = table[jax.random.permutation(jax.random.fold_in(own, 1), rows)]
    offset_by = jax.random.randint(jax.random.fold_in(own, 2), (rows, 1), 0, top)
    return jnp.take_along_axis(table, (jnp.arange(top)[None, :] + offset_by) % top, axis=1)


def load_shares(number_of, total, reach, slope, full):
    loads = [(1 << 20) // math.isqrt(rank ** slope) + 1 for rank in range(1, number_of + 1)]
    largest = reach if full else min(reach, max(-(-total // number_of), total * loads[0] // sum(loads)))
    least = 1 if total - largest >= number_of - 1 else 0
    given, spare = [largest] + [least] * (number_of - 1), total - largest - least * (number_of - 1)
    while spare > 0:
        candidates = [i for i in range(1, number_of) if given[i] < largest] or [i for i in range(1, number_of) if given[i] < reach]
        whole, budget = sum([loads[i] for i in candidates]), spare
        for i in candidates:
            more = min(reach - given[i], max(1, budget * loads[i] // whole), spare)
            given[i] = given[i] + more
            spare = spare - more
    return np.array(given)


def scatter_about(stream_key, dims, deviation, reach, cuts=(), kind=jnp.bfloat16):
    factor_of = steps_of(stream_key, dims, cuts, -0.22, 0.18) if cuts else 1.0
    drawn = jax.random.normal(stream_key, dims, jnp.float32) * deviation * factor_of
    return jnp.minimum(jnp.maximum(drawn, -reach), reach).astype(kind)


def setup_inputs(seed: int = 0) -> dict:
    arg_keys = jax.random.split(jax.random.key(seed), 10)
    hidden_rows = draw_hidden_rows(jax.random.fold_in(arg_keys[9], 71), 0)
    norm_gain = jnp.clip(1.0 + 0.1 * jax.random.normal(arg_keys[1], (D,), jnp.float32), 0.5, 1.5)
    router_weight = scatter_about(arg_keys[2], (D, EXPERTS), (D // 4) ** -0.5, 0.25)
    expert_ids_keys = jax.random.split(jax.random.fold_in(arg_keys[3], 1), TOKENS // MB_TOK)
    expert_ids_turns = jax.random.permutation(jax.random.fold_in(arg_keys[3], 3), TOKENS // MB_TOK)
    expert_ids = jax.vmap(lambda own, number: shared_out(jax.random.fold_in(arg_keys[3], 2), own, number, MB_TOK, EXPERTS, TOPK, CAP, 1))(expert_ids_keys, expert_ids_turns).reshape((TOKENS, TOPK))
    gate_weight = scatter_about(arg_keys[4], (N_SEGMENT, N_EXP, HALF, D), D ** -0.5, 0.125, ((0, 4), (1, 32)))
    up_weight = scatter_about(arg_keys[5], (N_SEGMENT, N_EXP, HALF, D), D ** -0.5, 0.125, ((0, 4), (1, 32)))
    down_weight = scatter_about(arg_keys[6], (N_SEGMENT, N_EXP, HALF, D), FF ** -0.5, 0.15625, ((0, 4), (1, 32)))
    latent_gain = jnp.clip(1.0 + 0.1 * jax.random.normal(arg_keys[7], (D,), jnp.float32), 0.5, 1.5)
    kv_weight = scatter_about(arg_keys[8], (D, KV_RANK), D ** -0.5, 0.125)
    return dict(hidden_rows=hidden_rows, norm_gain=norm_gain, router_weight=router_weight, expert_ids=expert_ids, gate_weight=gate_weight, up_weight=up_weight, down_weight=down_weight, latent_gain=latent_gain, kv_weight=kv_weight)


def rms_norm(values, gain):
    mean_square = lax.optimization_barrier(jnp.mean(values * values, axis=-1, keepdims=True))
    return values * lax.rsqrt(mean_square + 1e-06) * gain

def reference(hidden_rows, norm_gain, router_weight, expert_ids, gate_weight, up_weight, down_weight, latent_gain, kv_weight):
    residual = hidden_rows.astype(jnp.float32)
    normed = rms_norm(residual, norm_gain).astype(jnp.bfloat16)
    logits = jnp.dot(normed, router_weight, preferred_element_type=jnp.float32)
    picked = jnp.take_along_axis(logits, expert_ids, axis=1)
    affinity = jax.nn.sigmoid(picked)
    gate_share = affinity / lax.optimization_barrier(jnp.sum(affinity, axis=1, keepdims=True))
    blocks = TOKENS // MB_TOK
    flat_ids = expert_ids.reshape(blocks, MB_TOK * TOPK)
    onehot = (flat_ids[:, :, None] == jnp.arange(EXPERTS, dtype=jnp.int32)[None, None, :]).astype(jnp.int32)
    slot_rank = lax.optimization_barrier(jnp.sum((jnp.cumsum(onehot, axis=1) - onehot) * onehot, axis=2))
    counts = lax.optimization_barrier(jnp.sum(onehot, axis=(0, 1)))
    position = (jnp.arange(blocks, dtype=jnp.int32)[:, None] * CAP + slot_rank).reshape(TOKENS, TOPK)
    slot_total = blocks * CAP
    token_index = jnp.broadcast_to(jnp.arange(TOKENS, dtype=jnp.int32)[:, None], (TOKENS, TOPK))
    token_row = jnp.full((EXPERTS, slot_total), TOKENS, jnp.int32).at[expert_ids, position].set(token_index)
    gate_table = jnp.zeros((EXPERTS, slot_total), jnp.float32).at[expert_ids, position].set(gate_share)
    padded_rows = jnp.concatenate([normed, jnp.zeros((1, D), jnp.bfloat16)], axis=0)

    def expert_step(mix_rows, inputs):
        expert, rows_index, gate_row, count = inputs
        pair_index = expert // N_EXP
        column = expert % N_EXP
        gate_full = jnp.concatenate([gate_weight[2 * pair_index, column], gate_weight[2 * pair_index + 1, column]], axis=0)
        up_full = jnp.concatenate([up_weight[2 * pair_index, column], up_weight[2 * pair_index + 1, column]], axis=0)
        down_full = jnp.concatenate([down_weight[2 * pair_index, column], down_weight[2 * pair_index + 1, column]], axis=0)
        expert_rows = padded_rows[rows_index]
        gate_pre = jnp.dot(expert_rows, gate_full.T, preferred_element_type=jnp.float32)
        up_pre = jnp.dot(expert_rows, up_full.T, preferred_element_type=jnp.float32)
        hidden = (jax.nn.silu(gate_pre) * up_pre).astype(jnp.bfloat16)
        output_rows = jnp.dot(hidden, down_full, preferred_element_type=jnp.float32)
        mix_rows = mix_rows.at[rows_index].add(output_rows * gate_row[:, None])
        inverse_count = 2.0 / count.astype(jnp.float32)
        gram_in = jnp.dot(expert_rows.T, expert_rows, preferred_element_type=jnp.float32) * inverse_count
        gram_hid = jnp.dot(hidden.T, hidden, preferred_element_type=jnp.float32) * inverse_count
        return (mix_rows, (gram_in, gram_hid))
    start_mix = jnp.zeros((TOKENS + 1, D), jnp.float32)
    mix_rows, grams = lax.scan(expert_step, start_mix, (jnp.arange(EXPERTS, dtype=jnp.int32), token_row, gate_table, counts))
    expert_mix = mix_rows[:TOKENS].astype(jnp.bfloat16)
    combined = residual + expert_mix.astype(jnp.float32)
    normed_next = rms_norm(combined, latent_gain).astype(jnp.bfloat16)
    latents = jnp.dot(normed_next, kv_weight, preferred_element_type=jnp.float32).astype(jnp.bfloat16)
    gram_input = grams[0].reshape(PAIRS, N_EXP, 2, D // 2, D).transpose(0, 2, 1, 3, 4).reshape(N_SEGMENT, N_EXP, D // 2, D)
    gram_hidden = grams[1].reshape(PAIRS, N_EXP, 2, HALF, FF).transpose(0, 2, 1, 3, 4).reshape(N_SEGMENT, N_EXP, HALF, FF)
    return (expert_mix, latents, gram_input, gram_hidden)
```

```python
import jax
import jax.numpy as jnp
from jax import lax
from jax.sharding import PartitionSpec as P


MB_TOK = 64
MATE, FAR, OUTER = 1, 2, 3
SIZES = (24, 16, 16)
RETURNS = ((0, 1), (2,))
MATE, FAR, OUTER = 1, 2, 3
SIZES = (24, 16, 16)
RETURNS = ((0, 1), (2,))
F32 = jnp.float32
BF16 = jnp.bfloat16


def swapped(value, mask):
    pairs = [(source, source ^ mask) for source in range(lax.axis_size("segment"))]
    return lax.ppermute(value, "segment", pairs)


def rms_norm(values, gain):
    mean_square = jnp.mean(values * values, axis=-1, keepdims=True)
    return values * lax.rsqrt(mean_square + 1e-06) * gain


def exchanged(value):
    return lax.all_to_all(value, "exp", split_axis=0, concat_axis=0, tiled=True)


def dot(left, right, dims):
    return lax.dot_general(left, right, (dims, ((), ())), preferred_element_type=F32)


def layer(
    hidden_rows,
    norm_gain,
    router_weight,
    expert_ids,
    gate_weight,
    up_weight,
    down_weight,
    latent_gain,
    kv_weight,
):
    columns = lax.axis_size("exp")
    model_width = hidden_rows.shape[1]
    width_half = model_width // 2
    experts = router_weight.shape[1]
    top_count = expert_ids.shape[1]
    rows = hidden_rows.shape[0]
    capacity = MB_TOK * top_count * 5 // (4 * experts)
    segment = lax.axis_index("segment")
    half = segment % 2
    pair = segment // 2
    w_gate = gate_weight[0, 0]
    w_up = up_weight[0, 0]
    w_down = down_weight[0, 0]
    half_units = w_gate.shape[0]

    residual = hidden_rows.astype(F32)
    normed = rms_norm(residual, norm_gain).astype(BF16)
    normed, ids_t = lax.optimization_barrier((normed, expert_ids.T))
    ids_mate = swapped(ids_t, MATE)
    rows_mate = swapped(normed, MATE)
    rows_outer = swapped(normed, OUTER)
    ids_outer = swapped(ids_t, OUTER)
    ids_far = swapped(ids_t, FAR)
    mid = rows // 2
    far_low = swapped(rows_outer[:mid], MATE)
    far_high = swapped(rows_mate[mid:], OUTER)
    tokens_pair = jnp.concatenate([normed, rows_mate], axis=0)
    tokens_far = jnp.concatenate([rows_outer, far_low, far_high], axis=0)
    tokens_all = jnp.concatenate([tokens_pair, tokens_far], axis=0)

    own_cols = lax.dynamic_slice_in_dim(w_down, half * width_half, width_half, 1)
    other_cols = lax.dynamic_slice_in_dim(w_down, (1 - half) * width_half, width_half, 1)
    other_cols, far_low, far_high = lax.optimization_barrier((other_cols, far_low, far_high))
    partner_cols = swapped(other_cols, MATE)
    first = half == 0
    down_cols = jnp.concatenate(
        [jnp.where(first, own_cols, partner_cols), jnp.where(first, partner_cols, own_cols)], axis=0
    )

    expert_grid = jnp.arange(experts, dtype=jnp.int32)
    own_grid = expert_grid[:columns] + pair * columns
    block = jnp.arange(rows, dtype=jnp.int32)
    earlier = (block[:, None] < block[None, :]) & (
        block[:, None] // MB_TOK == block[None, :] // MB_TOK
    )
    earlier = earlier.astype(BF16)

    def slots_of(ids, position):
        chosen = jnp.any(ids[:, None, :] == own_grid[None, :, None], axis=0)
        rank = dot(chosen.astype(BF16), earlier, ((1,), (0,))).astype(jnp.int32)
        base = capacity * (block // MB_TOK + position * (rows // MB_TOK))
        return jnp.where(chosen, rank + base[None, :], -1)

    slot_pair = jnp.concatenate([slots_of(ids_t, half), slots_of(ids_mate, 1 - half)], axis=1)
    slot_pair_late, ids_outer, ids_far = lax.optimization_barrier((slot_pair, ids_outer, ids_far))
    slot_far = jnp.concatenate([slots_of(ids_outer, 3 - half), slots_of(ids_far, 2 + half)], axis=1)
    slot_all = jnp.concatenate([slot_pair_late, slot_far], axis=1)
    ids_all = jnp.concatenate([ids_t, ids_mate, ids_outer, ids_far], axis=1)

    def hits(slot, low, size):
        grid = low + jnp.arange(size, dtype=jnp.int32)
        return slot[:, None, :] == grid[None, :, None]

    chosen = jnp.any(ids_all[:, None, :] == expert_grid[None, :, None], axis=0)
    logits_t = dot(router_weight, tokens_all, ((0,), (1,)))
    affinity = jnp.where(chosen, jax.nn.sigmoid(logits_t), 0.0)
    share_all = affinity / jnp.sum(affinity, axis=0, keepdims=True)
    share = lax.dynamic_slice_in_dim(share_all, pair * columns, columns, 0)

    lows = [sum(SIZES[:i]) for i in range(len(SIZES))]
    sides = ((slot_pair, tokens_pair), (slot_all, tokens_all), (slot_far, tokens_far))
    counts = jnp.sum((slot_all >= 0).astype(F32), axis=1)
    last = len(SIZES) - 1
    received = []
    count_total = None
    for index, (low, size) in enumerate(zip(lows, SIZES)):
        slot, tokens = sides[index]
        picks = hits(slot, low, size).astype(BF16).reshape(columns * size, slot.shape[1])
        buffer = dot(picks, tokens, ((1,), (0,))).astype(BF16)
        buffer = buffer.reshape(columns, size, model_width)
        if index == last:
            extra = jnp.broadcast_to(counts.astype(BF16)[:, None, None], (columns, size, 128))
            buffer = jnp.concatenate([buffer, extra], axis=2)
        if index:
            buffer, received[-1] = lax.optimization_barrier((buffer, received[-1]))
        if index == last:
            arrived = exchanged(buffer)
            count_total = jnp.sum(arrived[:, 0, model_width].astype(F32))
            arrived = arrived[:, :, :model_width]
        else:
            arrived = exchanged(buffer)
        received.append(arrived.reshape(columns * size, model_width))
    hidden, full, outs = [], [], []
    for index, value in enumerate(received):
        gate_pre = dot(w_gate, value, ((1,), (1,)))
        up_pre = dot(w_up, value, ((1,), (1,)))
        own_t = (jax.nn.silu(gate_pre) * up_pre).astype(BF16)
        other_t = swapped(own_t, MATE)
        if index == 0:
            other_t, received[1] = lax.optimization_barrier((other_t, received[1]))
        full_t = jnp.concatenate(
            [jnp.where(first, own_t, other_t), jnp.where(first, other_t, own_t)], axis=0
        )
        out = dot(full_t, down_cols, ((0,), (0,))).astype(BF16)
        hidden.append(own_t)
        full.append(full_t)
        outs.append(out.reshape(columns, -1, width_half))

    mixes, backs, tables = [], [], []
    for group, slot, part in ((RETURNS[0], slot_all, share), (RETURNS[1], slot_far, share[:, 2 * rows :])):
        low, size = lows[group[0]], sum(SIZES[i] for i in group)
        sent = jnp.concatenate([outs[i] for i in group], axis=1)
        if backs:
            sent, backs[-1] = lax.optimization_barrier((sent, backs[-1]))
        else:
            sent, count_total = lax.optimization_barrier((sent, count_total))
        back = exchanged(sent)
        backs.append(back)
        tables.append((low, size, slot, part))
    for back, (low, size, slot, part) in zip(backs, tables):
        back = back.reshape(columns * size, width_half)
        table = jnp.where(hits(slot, low, size), part[:, None, :], 0.0)
        table = table.reshape(columns * size, slot.shape[1])
        high_part = table.astype(BF16)
        low_part = (table - high_part.astype(F32)).astype(BF16)
        mixes.append(dot(high_part, back, ((0,), (0,))) + dot(low_part, back, ((0,), (0,))))
    mix_own = mixes[0][:rows]
    mix_mate = mixes[0][rows : 2 * rows]
    mix_far = mixes[0][2 * rows :] + mixes[1]
    from_mate = swapped(mix_mate.astype(BF16), MATE)
    from_outer = swapped(mix_far[:rows].astype(BF16), OUTER)
    from_far = swapped(mix_far[rows:].astype(BF16), FAR)
    mine = mix_own + from_far.astype(F32)
    others = from_mate.astype(F32) + from_outer.astype(F32)
    expert_mix = jnp.concatenate(
        [jnp.where(first, mine, others), jnp.where(first, others, mine)], axis=1
    ).astype(BF16)
    combined = residual + expert_mix.astype(F32)
    normed_next = rms_norm(combined, latent_gain).astype(BF16)
    latents = jnp.dot(normed_next, kv_weight, preferred_element_type=F32).astype(BF16)

    inverse_count = 2.0 / count_total
    gram_in = jnp.zeros((width_half, model_width), F32)
    gram_hid = jnp.zeros((half_units, 2 * half_units), F32)
    for index, (value, own_t, full_t) in enumerate(zip(received, hidden, full)):
        if index:
            value, own_t, full_t, inverse_count = lax.optimization_barrier(
                (value, own_t, full_t, inverse_count)
            )
        own_part = lax.dynamic_slice_in_dim(value, half * width_half, width_half, 1)
        gram_in = gram_in + dot(own_part, value, ((0,), (0,)))
        gram_hid = gram_hid + dot(own_t, full_t, ((1,), (1,)))
    gram_input = (gram_in * inverse_count)[None, None]
    gram_hidden = (gram_hid * inverse_count)[None, None]
    return (expert_mix, latents, gram_input, gram_hidden)


def solution(mesh):
    return jax.shard_map(
        layer,
        mesh=mesh,
        in_specs=(
            P(("segment", "exp"), None),
            P(),
            P(),
            P(("segment", "exp"), None),
            P("segment", "exp", None, None),
            P("segment", "exp", None, None),
            P("segment", "exp", None, None),
            P(),
            P(),
        ),
        out_specs=(
            P(("segment", "exp"), None),
            P(("segment", "exp"), None),
            P("segment", "exp", None, None),
            P("segment", "exp", None, None),
        ),
        check_vma=False,
    )
```

```python
import jax
import jax.numpy as jnp
from jax import lax
from jax.sharding import PartitionSpec as P


MB_TOK = 64
MATE, FAR, OUTER = 1, 2, 3
SIZES = (16, 24, 16)
RETURNS = ((0, 1), (2,))
MATE, FAR, OUTER = 1, 2, 3
SIZES = (16, 24, 16)
RETURNS = ((0, 1), (2,))
F32 = jnp.float32
BF16 = jnp.bfloat16


def swapped(value, mask):
    pairs = [(source, source ^ mask) for source in range(lax.axis_size("segment"))]
    return lax.ppermute(value, "segment", pairs)


def rms_norm(values, gain):
    mean_square = jnp.mean(values * values, axis=-1, keepdims=True)
    return values * lax.rsqrt(mean_square + 1e-06) * gain


def exchanged(value):
    return lax.all_to_all(value, "exp", split_axis=0, concat_axis=0, tiled=True)


def dot(left, right, dims):
    return lax.dot_general(left, right, (dims, ((), ())), preferred_element_type=F32)


def layer(
    hidden_rows,
    norm_gain,
    router_weight,
    expert_ids,
    gate_weight,
    up_weight,
    down_weight,
    latent_gain,
    kv_weight,
):
    columns = lax.axis_size("exp")
    model_width = hidden_rows.shape[1]
    width_half = model_width // 2
    experts = router_weight.shape[1]
    top_count = expert_ids.shape[1]
    rows = hidden_rows.shape[0]
    capacity = MB_TOK * top_count * 5 // (4 * experts)
    segment = lax.axis_index("segment")
    half = segment % 2
    pair = segment // 2
    w_gate = gate_weight[0, 0]
    w_up = up_weight[0, 0]
    w_down = down_weight[0, 0]
    half_units = w_gate.shape[0]

    residual = hidden_rows.astype(F32)
    normed = rms_norm(residual, norm_gain).astype(BF16)
    normed, ids_t = lax.optimization_barrier((normed, expert_ids.T))
    first = half == 0
    mine_at, other_at = half * width_half, (1 - half) * width_half

    def columns_at(value, start):
        return lax.dynamic_slice_in_dim(value, start, width_half, 1)

    def joined(mine, other):
        return jnp.concatenate(
            [jnp.where(first, mine, other), jnp.where(first, other, mine)], axis=1
        )

    ids_mate = swapped(ids_t, MATE)
    normed_mine, normed_other = columns_at(normed, mine_at), columns_at(normed, other_at)
    mate_mine = swapped(normed_other, MATE)
    rows_outer = swapped(normed, OUTER)
    mate_other = swapped(normed_mine, MATE)
    ids_outer = swapped(ids_t, OUTER)
    ids_far = swapped(ids_t, FAR)
    rows_mate = joined(mate_mine, mate_other)
    tokens_mine = jnp.concatenate([normed_mine, mate_mine], axis=0)
    mid = rows // 2
    far_low = swapped(rows_outer[:mid], MATE)
    far_high = swapped(rows_mate[mid:], OUTER)
    tokens_pair = jnp.concatenate([normed, rows_mate], axis=0)
    tokens_far = jnp.concatenate([rows_outer, far_low, far_high], axis=0)
    tokens_all = jnp.concatenate([tokens_pair, tokens_far], axis=0)

    own_cols = columns_at(w_down, mine_at)
    other_cols = columns_at(w_down, other_at)
    other_cols, far_low, far_high = lax.optimization_barrier((other_cols, far_low, far_high))
    split = half_units // 2
    partner_a = swapped(other_cols[:split], MATE)
    partner_b = swapped(other_cols[split:], MATE)
    partner_cols = jnp.concatenate([partner_a, partner_b], axis=0)
    down_cols = jnp.concatenate(
        [jnp.where(first, own_cols, partner_cols), jnp.where(first, partner_cols, own_cols)], axis=0
    )

    expert_grid = jnp.arange(experts, dtype=jnp.int32)
    own_grid = expert_grid[:columns] + pair * columns
    block = jnp.arange(rows, dtype=jnp.int32)
    earlier = (block[:, None] < block[None, :]) & (
        block[:, None] // MB_TOK == block[None, :] // MB_TOK
    )
    earlier = earlier.astype(BF16)

    def slots_of(ids, position):
        chosen = jnp.any(ids[:, None, :] == own_grid[None, :, None], axis=0)
        rank = dot(chosen.astype(BF16), earlier, ((1,), (0,))).astype(jnp.int32)
        base = capacity * (block // MB_TOK + position * (rows // MB_TOK))
        return jnp.where(chosen, rank + base[None, :], -1)

    slot_pair = jnp.concatenate([slots_of(ids_t, half), slots_of(ids_mate, 1 - half)], axis=1)
    slot_pair_late, ids_outer, ids_far = lax.optimization_barrier((slot_pair, ids_outer, ids_far))
    slot_far = jnp.concatenate([slots_of(ids_outer, 3 - half), slots_of(ids_far, 2 + half)], axis=1)
    slot_all = jnp.concatenate([slot_pair_late, slot_far], axis=1)
    ids_all = jnp.concatenate([ids_t, ids_mate, ids_outer, ids_far], axis=1)

    def hits(slot, low, size):
        grid = low + jnp.arange(size, dtype=jnp.int32)
        return slot[:, None, :] == grid[None, :, None]

    chosen = jnp.any(ids_all[:, None, :] == expert_grid[None, :, None], axis=0)
    logits_t = dot(router_weight, tokens_all, ((0,), (1,)))
    affinity = jnp.where(chosen, jax.nn.sigmoid(logits_t), 0.0)
    share_all = affinity / jnp.sum(affinity, axis=0, keepdims=True)
    share = lax.dynamic_slice_in_dim(share_all, pair * columns, columns, 0)

    lows = [sum(SIZES[:i]) for i in range(len(SIZES))]
    sides = ((slot_pair, tokens_mine), (slot_all, tokens_all), (slot_far, tokens_far))
    counts = jnp.sum((slot_all >= 0).astype(F32), axis=1)
    last = len(SIZES) - 1
    received = []
    count_total = None
    for index, (low, size) in enumerate(zip(lows, SIZES)):
        slot, tokens = sides[index]
        picks = hits(slot, low, size).astype(BF16).reshape(columns * size, slot.shape[1])
        buffer = dot(picks, tokens, ((1,), (0,))).astype(BF16)
        buffer = buffer.reshape(columns, size, -1)
        if index == last:
            extra = jnp.broadcast_to(counts.astype(BF16)[:, None, None], (columns, size, 128))
            buffer = jnp.concatenate([buffer, extra], axis=2)
        if index:
            buffer, received[-1] = lax.optimization_barrier((buffer, received[-1]))
        if index == last:
            arrived = exchanged(buffer)
            count_total = jnp.sum(arrived[:, 0, model_width].astype(F32))
            arrived = arrived[:, :, :model_width]
        else:
            arrived = exchanged(buffer)
        if index == 0:
            mine = arrived.reshape(columns * size, width_half)
            other = swapped(mine, MATE)
        received.append(mine if index == 0 else arrived.reshape(columns * size, model_width))
    received[0] = joined(received[0], other)
    hidden, full, outs = [], [], []
    for index, value in enumerate(received):
        gate_pre = dot(w_gate, value, ((1,), (1,)))
        up_pre = dot(w_up, value, ((1,), (1,)))
        own_t = (jax.nn.silu(gate_pre) * up_pre).astype(BF16)
        other_t = swapped(own_t, MATE)
        if index == 0:
            other_t, received[1] = lax.optimization_barrier((other_t, received[1]))
        full_t = jnp.concatenate(
            [jnp.where(first, own_t, other_t), jnp.where(first, other_t, own_t)], axis=0
        )
        out = dot(full_t, down_cols, ((0,), (0,))).astype(BF16)
        hidden.append(own_t)
        full.append(full_t)
        outs.append(out.reshape(columns, -1, width_half))

    mixes, backs, tables = [], [], []
    for group, slot, part in ((RETURNS[0], slot_all, share), (RETURNS[1], slot_far, share[:, 2 * rows :])):
        low, size = lows[group[0]], sum(SIZES[i] for i in group)
        sent = jnp.concatenate([outs[i] for i in group], axis=1)
        if backs:
            sent, backs[-1] = lax.optimization_barrier((sent, backs[-1]))
        else:
            sent, count_total = lax.optimization_barrier((sent, count_total))
        back = exchanged(sent)
        backs.append(back)
        tables.append((low, size, slot, part))
    for back, (low, size, slot, part) in zip(backs, tables):
        back = back.reshape(columns * size, width_half)
        table = jnp.where(hits(slot, low, size), part[:, None, :], 0.0)
        table = table.reshape(columns * size, slot.shape[1])
        high_part = table.astype(BF16)
        low_part = (table - high_part.astype(F32)).astype(BF16)
        mixes.append(dot(high_part, back, ((0,), (0,))) + dot(low_part, back, ((0,), (0,))))
    mix_own = mixes[0][:rows]
    mix_mate = mixes[0][rows : 2 * rows]
    mix_far = mixes[0][2 * rows :] + mixes[1]
    from_mate = swapped(mix_mate.astype(BF16), MATE)
    from_outer = swapped(mix_far[:rows].astype(BF16), OUTER)
    from_far = swapped(mix_far[rows:].astype(BF16), FAR)
    mine = mix_own + from_far.astype(F32)
    others = from_mate.astype(F32) + from_outer.astype(F32)
    expert_mix = jnp.concatenate(
        [jnp.where(first, mine, others), jnp.where(first, others, mine)], axis=1
    ).astype(BF16)
    combined = residual + expert_mix.astype(F32)
    normed_next = rms_norm(combined, latent_gain).astype(BF16)
    latents = jnp.dot(normed_next, kv_weight, preferred_element_type=F32).astype(BF16)

    inverse_count = 2.0 / count_total
    gram_in = jnp.zeros((width_half, model_width), F32)
    gram_hid = jnp.zeros((half_units, 2 * half_units), F32)
    for index, (value, own_t, full_t) in enumerate(zip(received, hidden, full)):
        if index:
            value, own_t, full_t, inverse_count = lax.optimization_barrier(
                (value, own_t, full_t, inverse_count)
            )
        own_part = lax.dynamic_slice_in_dim(value, half * width_half, width_half, 1)
        gram_in = gram_in + dot(own_part, value, ((0,), (0,)))
        gram_hid = gram_hid + dot(own_t, full_t, ((1,), (1,)))
    gram_input = (gram_in * inverse_count)[None, None]
    gram_hidden = (gram_hid * inverse_count)[None, None]
    return (expert_mix, latents, gram_input, gram_hidden)


def solution(mesh):
    return jax.shard_map(
        layer,
        mesh=mesh,
        in_specs=(
            P(("segment", "exp"), None),
            P(),
            P(),
            P(("segment", "exp"), None),
            P("segment", "exp", None, None),
            P("segment", "exp", None, None),
            P("segment", "exp", None, None),
            P(),
            P(),
        ),
        out_specs=(
            P(("segment", "exp"), None),
            P(("segment", "exp"), None),
            P("segment", "exp", None, None),
            P("segment", "exp", None, None),
        ),
        check_vma=False,
    )
```

```python
import jax
import jax.numpy as jnp
from jax import lax
from jax.sharding import PartitionSpec as P


MB_TOK = 64
MATE, FAR, OUTER = 1, 2, 3
SIZES = (24, 24, 8)
RETURNS = ((0,), (1, 2))
F32 = jnp.float32
BF16 = jnp.bfloat16


def swapped(value, mask):
    pairs = [(source, source ^ mask) for source in range(lax.axis_size("segment"))]
    return lax.ppermute(value, "segment", pairs)


def rms_norm(values, gain):
    mean_square = jnp.mean(values * values, axis=-1, keepdims=True)
    return values * lax.rsqrt(mean_square + 1e-06) * gain


def exchanged(value):
    return lax.all_to_all(value, "exp", split_axis=0, concat_axis=0, tiled=True)


def dot(left, right, dims):
    return lax.dot_general(left, right, (dims, ((), ())), preferred_element_type=F32)


def layer(
    hidden_rows,
    norm_gain,
    router_weight,
    expert_ids,
    gate_weight,
    up_weight,
    down_weight,
    latent_gain,
    kv_weight,
):
    columns = lax.axis_size("exp")
    model_width = hidden_rows.shape[1]
    width_half = model_width // 2
    experts = router_weight.shape[1]
    top_count = expert_ids.shape[1]
    rows = hidden_rows.shape[0]
    capacity = MB_TOK * top_count * 5 // (4 * experts)
    segment = lax.axis_index("segment")
    half = segment % 2
    pair = segment // 2
    w_gate = gate_weight[0, 0]
    w_up = up_weight[0, 0]
    w_down = down_weight[0, 0]
    half_units = w_gate.shape[0]

    residual = hidden_rows.astype(F32)
    normed = rms_norm(residual, norm_gain).astype(BF16)
    normed, ids_t = lax.optimization_barrier((normed, expert_ids.T))
    ids_mate = swapped(ids_t, MATE)
    rows_mate = swapped(normed, MATE)
    rows_outer = swapped(normed, OUTER)
    ids_outer = swapped(ids_t, OUTER)
    ids_far = swapped(ids_t, FAR)
    mid = rows // 2
    far_low = swapped(rows_outer[:mid], MATE)
    far_high = swapped(rows_mate[mid:], OUTER)
    tokens_pair = jnp.concatenate([normed, rows_mate], axis=0)
    tokens_far = jnp.concatenate([rows_outer, far_low, far_high], axis=0)
    tokens_all = jnp.concatenate([tokens_pair, tokens_far], axis=0)

    own_cols = lax.dynamic_slice_in_dim(w_down, half * width_half, width_half, 1)
    other_cols = lax.dynamic_slice_in_dim(w_down, (1 - half) * width_half, width_half, 1)
    other_cols, far_low, far_high = lax.optimization_barrier((other_cols, far_low, far_high))
    partner_cols = swapped(other_cols, MATE)
    first = half == 0
    down_cols = jnp.concatenate(
        [jnp.where(first, own_cols, partner_cols), jnp.where(first, partner_cols, own_cols)], axis=0
    )

    expert_grid = jnp.arange(experts, dtype=jnp.int32)
    own_grid = expert_grid[:columns] + pair * columns
    block = jnp.arange(rows, dtype=jnp.int32)
    earlier = (block[:, None] < block[None, :]) & (
        block[:, None] // MB_TOK == block[None, :] // MB_TOK
    )
    earlier = earlier.astype(BF16)

    def slots_of(ids, position):
        chosen = jnp.any(ids[:, None, :] == own_grid[None, :, None], axis=0)
        rank = dot(chosen.astype(BF16), earlier, ((1,), (0,))).astype(jnp.int32)
        base = capacity * (block // MB_TOK + position * (rows // MB_TOK))
        return jnp.where(chosen, rank + base[None, :], -1)

    slot_pair = jnp.concatenate([slots_of(ids_t, half), slots_of(ids_mate, 1 - half)], axis=1)
    slot_late, ids_outer, ids_far = lax.optimization_barrier((slot_pair, ids_outer, ids_far))
    slot_far = jnp.concatenate([slots_of(ids_outer, 3 - half), slots_of(ids_far, 2 + half)], axis=1)
    slot_all = jnp.concatenate([slot_late, slot_far], axis=1)
    ids_all = jnp.concatenate([ids_t, ids_mate, ids_outer, ids_far], axis=1)

    def hits(slot, low, size):
        grid = low + jnp.arange(size, dtype=jnp.int32)
        return slot[:, None, :] == grid[None, :, None]

    chosen = jnp.any(ids_all[:, None, :] == expert_grid[None, :, None], axis=0)
    logits_t = dot(router_weight, tokens_all, ((0,), (1,)))
    affinity = jnp.where(chosen, jax.nn.sigmoid(logits_t), 0.0)
    share_all = affinity / jnp.sum(affinity, axis=0, keepdims=True)
    share = lax.dynamic_slice_in_dim(share_all, pair * columns, columns, 0)

    lows = [sum(SIZES[:i]) for i in range(len(SIZES))]
    sides = ((slot_pair, tokens_pair), (slot_all, tokens_all), (slot_far, tokens_far))
    counts = jnp.sum((slot_all >= 0).astype(F32), axis=1)
    last = len(SIZES) - 1
    received = []
    count_total = None
    for index, (low, size) in enumerate(zip(lows, SIZES)):
        slot, tokens = sides[index]
        picks = hits(slot, low, size).astype(BF16).reshape(columns * size, slot.shape[1])
        buffer = dot(picks, tokens, ((1,), (0,))).astype(BF16)
        buffer = buffer.reshape(columns, size, model_width)
        if index == last:
            extra = jnp.broadcast_to(counts.astype(BF16)[:, None, None], (columns, size, 128))
            buffer = jnp.concatenate([buffer, extra], axis=2)
        if index == last:
            arrived = exchanged(buffer)
            count_total = jnp.sum(arrived[:, 0, model_width].astype(F32))
            arrived = arrived[:, :, :model_width]
        else:
            arrived = exchanged(buffer)
        received.append(arrived.reshape(columns * size, model_width))
    hidden, full, outs = [], [], []
    for value in received:
        gate_pre = dot(w_gate, value, ((1,), (1,)))
        up_pre = dot(w_up, value, ((1,), (1,)))
        own_t = (jax.nn.silu(gate_pre) * up_pre).astype(BF16)
        other_t = swapped(own_t, MATE)
        full_t = jnp.concatenate(
            [jnp.where(first, own_t, other_t), jnp.where(first, other_t, own_t)], axis=0
        )
        out = dot(full_t, down_cols, ((0,), (0,))).astype(BF16)
        hidden.append(own_t)
        full.append(full_t)
        outs.append(out.reshape(columns, -1, width_half))

    late = [jnp.concatenate([t[:, mid:rows], t[:, rows + mid :]], axis=1) for t in (slot_all, share)]
    mixes = []
    for group, slot, part in ((RETURNS[0], slot_pair, share[:, : 2 * rows]), (RETURNS[1], *late)):
        low, size = lows[group[0]], sum(SIZES[i] for i in group)
        sent = jnp.concatenate([outs[i] for i in group], axis=1)
        back = exchanged(sent)
        back = back.reshape(columns * size, width_half)
        table = jnp.where(hits(slot, low, size), part[:, None, :], 0.0)
        table = table.reshape(columns * size, slot.shape[1])
        mixes.append(dot(table.astype(BF16), back, ((0,), (0,))))
    mix_own = mixes[0][:rows] + jnp.pad(mixes[1][:mid], ((mid, 0), (0, 0)))
    mix_mate = mixes[0][rows:] + jnp.pad(mixes[1][mid:rows], ((mid, 0), (0, 0)))
    mix_far = mixes[1][rows:]
    from_far = swapped(mix_far[rows:].astype(BF16), FAR)
    from_outer = swapped(mix_far[:rows].astype(BF16), OUTER)
    from_mate = swapped(mix_mate.astype(BF16), MATE)
    mine = mix_own + from_far.astype(F32)
    others = from_mate.astype(F32) + from_outer.astype(F32)
    expert_mix = jnp.concatenate(
        [jnp.where(first, mine, others), jnp.where(first, others, mine)], axis=1
    ).astype(BF16)
    combined = residual + expert_mix.astype(F32)
    normed_next = rms_norm(combined, latent_gain).astype(BF16)
    latents = jnp.dot(normed_next, kv_weight, preferred_element_type=F32).astype(BF16)

    inverse_count = 2.0 / count_total
    gram_in = jnp.zeros((width_half, model_width), F32)
    gram_hid = jnp.zeros((half_units, 2 * half_units), F32)
    for index, (value, own_t, full_t) in enumerate(zip(received, hidden, full)):
        if index:
            value, own_t, full_t, inverse_count = lax.optimization_barrier(
                (value, own_t, full_t, inverse_count)
            )
        own_part = lax.dynamic_slice_in_dim(value, half * width_half, width_half, 1)
        gram_in = gram_in + dot(own_part, value, ((0,), (0,)))
        gram_hid = gram_hid + dot(own_t, full_t, ((1,), (1,)))
    gram_input = (gram_in * inverse_count)[None, None]
    gram_hidden = (gram_hid * inverse_count)[None, None]
    return (expert_mix, latents, gram_input, gram_hidden)


def solution(mesh):
    return jax.shard_map(
        layer,
        mesh=mesh,
        in_specs=(
            P(("segment", "exp"), None),
            P(),
            P(),
            P(("segment", "exp"), None),
            P("segment", "exp", None, None),
            P("segment", "exp", None, None),
            P("segment", "exp", None, None),
            P(),
            P(),
        ),
        out_specs=(
            P(("segment", "exp"), None),
            P(("segment", "exp"), None),
            P("segment", "exp", None, None),
            P("segment", "exp", None, None),
        ),
        check_vma=False,
    )
```

```python
import functools

import jax
import jax.numpy as jnp
from jax import lax
from jax.experimental import pallas as pl
from jax.experimental.pallas import tpu as pltpu
from jax.sharding import PartitionSpec as P


MB_TOK = 64
MATE, FAR, OUTER = 1, 2, 3
SIZES = (24, 16, 16)
RETURNS = ((0, 1), (2,))
F32 = jnp.float32
BF16 = jnp.bfloat16


def swapped(value, mask):
    pairs = [(source, source ^ mask) for source in range(lax.axis_size("segment"))]
    return lax.ppermute(value, "segment", pairs)


def rms_norm(values, gain):
    mean_square = jnp.mean(values * values, axis=-1, keepdims=True)
    return values * lax.rsqrt(mean_square + 1e-06) * gain


def exchanged(value):
    return lax.all_to_all(value, "exp", split_axis=0, concat_axis=0, tiled=True)


def dot(left, right, dims):
    return lax.dot_general(left, right, (dims, ((), ())), preferred_element_type=F32)


def layer(
    hidden_rows,
    norm_gain,
    router_weight,
    expert_ids,
    gate_weight,
    up_weight,
    down_weight,
    latent_gain,
    kv_weight,
):
    columns = lax.axis_size("exp")
    model_width = hidden_rows.shape[1]
    width_half = model_width // 2
    experts = router_weight.shape[1]
    top_count = expert_ids.shape[1]
    rows = hidden_rows.shape[0]
    capacity = MB_TOK * top_count * 5 // (4 * experts)
    segment = lax.axis_index("segment")
    half = segment % 2
    pair = segment // 2
    w_gate = gate_weight[0, 0]
    w_up = up_weight[0, 0]
    w_down = down_weight[0, 0]

    residual = hidden_rows.astype(F32)
    normed = rms_norm(residual, norm_gain).astype(BF16)
    normed, ids_t = lax.optimization_barrier((normed, expert_ids.T))
    ids_mate = swapped(ids_t, MATE)
    rows_mate = swapped(normed, MATE)
    rows_outer = swapped(normed, OUTER)
    ids_outer = swapped(ids_t, OUTER)
    ids_far = swapped(ids_t, FAR)
    mid = rows // 2
    far_low = swapped(rows_outer[:mid], MATE)
    far_high = swapped(rows_mate[mid:], OUTER)
    tokens_pair = jnp.concatenate([normed, rows_mate], axis=0)
    tokens_far = jnp.concatenate([rows_outer, far_low, far_high], axis=0)
    tokens_all = jnp.concatenate([tokens_pair, tokens_far], axis=0)

    own_cols = lax.dynamic_slice_in_dim(w_down, half * width_half, width_half, 1)
    other_cols = lax.dynamic_slice_in_dim(w_down, (1 - half) * width_half, width_half, 1)
    other_cols, far_low, far_high = lax.optimization_barrier((other_cols, far_low, far_high))
    partner_cols = swapped(other_cols, MATE)
    first = half == 0
    down_cols = jnp.concatenate(
        [jnp.where(first, own_cols, partner_cols), jnp.where(first, partner_cols, own_cols)],
        axis=0,
    )

    expert_grid = jnp.arange(experts, dtype=jnp.int32)
    own_grid = expert_grid[:columns] + pair * columns
    block = jnp.arange(rows, dtype=jnp.int32)
    earlier = (block[:, None] < block[None, :]) & (
        block[:, None] // MB_TOK == block[None, :] // MB_TOK
    )
    earlier = earlier.astype(BF16)

    def slots_of(ids, position):
        chosen = jnp.any(ids[:, None, :] == own_grid[None, :, None], axis=0)
        rank = dot(chosen.astype(BF16), earlier, ((1,), (0,))).astype(jnp.int32)
        base = capacity * (block // MB_TOK + position * (rows // MB_TOK))
        return jnp.where(chosen, rank + base[None, :], -1)

    slot_pair = jnp.concatenate([slots_of(ids_t, half), slots_of(ids_mate, 1 - half)], axis=1)
    slot_late, ids_outer, ids_far = lax.optimization_barrier((slot_pair, ids_outer, ids_far))
    slot_far = jnp.concatenate([slots_of(ids_outer, 3 - half), slots_of(ids_far, 2 + half)], axis=1)
    slot_all = jnp.concatenate([slot_late, slot_far], axis=1)
    ids_all = jnp.concatenate([ids_t, ids_mate, ids_outer, ids_far], axis=1)

    def hits(slot, low, size):
        grid = low + jnp.arange(size, dtype=jnp.int32)
        return slot[:, None, :] == grid[None, :, None]

    chosen = jnp.any(ids_all[:, None, :] == expert_grid[None, :, None], axis=0)
    logits_t = dot(router_weight, tokens_all, ((0,), (1,)))
    affinity = jnp.where(chosen, jax.nn.sigmoid(logits_t), 0.0)
    share_all = affinity / jnp.sum(affinity, axis=0, keepdims=True)
    share = lax.dynamic_slice_in_dim(share_all, pair * columns, columns, 0)

    lows = [sum(SIZES[:i]) for i in range(len(SIZES))]
    sides = ((slot_pair, tokens_pair), (slot_all, tokens_all), (slot_far, tokens_far))
    counts = jnp.sum((slot_all >= 0).astype(F32), axis=1)
    last = len(SIZES) - 1
    received = []
    count_total = None
    for index, (low, size) in enumerate(zip(lows, SIZES)):
        slot, tokens = sides[index]
        picks = hits(slot, low, size).astype(BF16).reshape(columns * size, slot.shape[1])
        buffer = dot(picks, tokens, ((1,), (0,))).astype(BF16)
        buffer = buffer.reshape(columns, size, model_width)
        if index == last:
            extra = jnp.broadcast_to(counts.astype(BF16)[:, None, None], (columns, size, 128))
            buffer = jnp.concatenate([buffer, extra], axis=2)
        if index == last:
            arrived = exchanged(buffer)
            count_total = jnp.sum(arrived[:, 0, model_width].astype(F32))
            arrived = arrived[:, :, :model_width]
        else:
            arrived = exchanged(buffer)
        received.append(arrived.reshape(columns * size, model_width))
    hidden, full, outs = [], [], []
    for value in received:
        gate_pre = dot(w_gate, value, ((1,), (1,)))
        up_pre = dot(w_up, value, ((1,), (1,)))
        own_t = (jax.nn.silu(gate_pre) * up_pre).astype(BF16)
        other_t = swapped(own_t, MATE)
        full_t = jnp.concatenate(
            [jnp.where(first, own_t, other_t), jnp.where(first, other_t, own_t)], axis=0
        )
        out = dot(full_t, down_cols, ((0,), (0,))).astype(BF16)
        hidden.append(own_t)
        full.append(full_t)
        outs.append(out.reshape(columns, -1, width_half))

    mixes = []
    for group, slot, part in ((RETURNS[0], slot_all, share), (RETURNS[1], slot_far, share[:, 2 * rows :])):
        low, size = lows[group[0]], sum(SIZES[i] for i in group)
        sent = jnp.concatenate([outs[i] for i in group], axis=1)
        back = exchanged(sent)
        back = back.reshape(columns * size, width_half)
        table = jnp.where(hits(slot, low, size), part[:, None, :], 0.0)
        table = table.reshape(columns * size, slot.shape[1])
        mixes.append(dot(table.astype(BF16), back, ((0,), (0,))))
    mix_own = mixes[0][:rows]
    mix_mate = mixes[0][rows : 2 * rows]
    mix_far = mixes[0][2 * rows :] + mixes[1]
    from_far = swapped(mix_far[rows:].astype(BF16), FAR)
    from_outer = swapped(mix_far[:rows].astype(BF16), OUTER)
    from_mate = swapped(mix_mate.astype(BF16), MATE)
    mine = mix_own + from_far.astype(F32)
    others = from_mate.astype(F32) + from_outer.astype(F32)
    expert_mix = jnp.concatenate(
        [jnp.where(first, mine, others), jnp.where(first, others, mine)], axis=1
    ).astype(BF16)
    combined = residual + expert_mix.astype(F32)
    normed_next = rms_norm(combined, latent_gain).astype(BF16)
    latents = jnp.dot(normed_next, kv_weight, preferred_element_type=F32).astype(BF16)

    inverse_count = 2.0 / count_total
    gram_first = hidden_gram(hidden[:1], full[:1])
    gram_hid = hidden_gram(hidden[1:], full[1:], gram_first, inverse_count)
    gram_in = scaled_gram(half, inverse_count, received, width_half)
    return (expert_mix, latents, gram_in[None, None], gram_hid[None, None])


def gram_kernel(half_ref, scale_ref, *refs):
    count = len(SIZES)
    left, right, out_ref, turned = refs[:count], refs[count : 2 * count], refs[-2], refs[-1]
    ends = [0]
    for ref in left:
        ends.append(ends[-1] + ref.shape[0])

    @pl.when(pl.program_id(1) == 0)
    def _():
        for ref, low, high in zip(left, ends, ends[1:]):
            turned[:, low:high] = ref[...].T

    total = None
    for ref, low, high in zip(right, ends, ends[1:]):
        part = dot(turned[:, low:high], ref[...], ((1,), (0,)))
        total = part if total is None else total + part
    out_ref[...] = total * scale_ref[0, 0]


def scaled_gram(half, scale, chunks, out_rows):
    width = chunks[0].shape[1]
    tile, wide = 512, 512
    steps = out_rows // tile
    left = [
        pl.BlockSpec((c.shape[0], tile), lambda i, j, half: (0, half[0] * steps + i)) for c in chunks
    ]
    right = [pl.BlockSpec((c.shape[0], wide), lambda i, j, half: (0, j)) for c in chunks]
    depth = sum(c.shape[0] for c in chunks)
    return pl.pallas_call(
        gram_kernel,
        grid_spec=pltpu.PrefetchScalarGridSpec(
            num_scalar_prefetch=1,
            grid=(steps, width // wide),
            in_specs=[pl.BlockSpec(memory_space=pltpu.SMEM), *left, *right],
            out_specs=pl.BlockSpec((tile, wide), lambda i, j, half: (i, j)),
            scratch_shapes=[pltpu.VMEM((tile, depth), BF16)],
        ),
        out_shape=jax.ShapeDtypeStruct((out_rows, width), F32),
        cost_estimate=pl.CostEstimate(
            flops=2 * depth * out_rows * width,
            transcendentals=0,
            bytes_accessed=4 * out_rows * width + 6 * depth * width,
        ),
    )(half.astype(jnp.int32).reshape(1), scale.reshape(1, 1), *chunks, *chunks)


def hidden_gram_kernel(count, *refs):
    own, full = refs[:count], refs[count : 2 * count]
    total = None
    for a_ref, b_ref in zip(own, full):
        part = dot(a_ref[...], b_ref[...], ((1,), (1,)))
        total = part if total is None else total + part
    if len(refs) > 2 * count + 1:
        base_ref, scale_ref = refs[2 * count : 2 * count + 2]
        total = (total + base_ref[...]) * scale_ref[0, 0]
    refs[-1][...] = total


def hidden_gram(own, full, base=None, scale=None):
    units, width = own[0].shape[0], full[0].shape[0]
    tile = 128
    depth = sum(v.shape[1] for v in own)
    out_spec = pl.BlockSpec((units, tile), lambda j: (0, j))
    operands = (*own, *full)
    specs = [
        *[pl.BlockSpec((units, v.shape[1]), lambda j: (0, 0)) for v in own],
        *[pl.BlockSpec((tile, v.shape[1]), lambda j: (j, 0)) for v in full],
    ]
    if base is not None:
        operands += (base, scale.reshape(1, 1))
        specs += [out_spec, pl.BlockSpec(memory_space=pltpu.SMEM)]
    return pl.pallas_call(
        functools.partial(hidden_gram_kernel, len(own)),
        grid=(width // tile,),
        in_specs=specs,
        out_specs=out_spec,
        out_shape=jax.ShapeDtypeStruct((units, width), F32),
        cost_estimate=pl.CostEstimate(
            flops=2 * depth * units * width,
            transcendentals=0,
            bytes_accessed=4 * units * width + 2 * depth * (units + width),
        ),
    )(*operands)


def solution(mesh):
    return jax.shard_map(
        layer,
        mesh=mesh,
        in_specs=(
            P(("segment", "exp"), None),
            P(),
            P(),
            P(("segment", "exp"), None),
            P("segment", "exp", None, None),
            P("segment", "exp", None, None),
            P("segment", "exp", None, None),
            P(),
            P(),
        ),
        out_specs=(
            P(("segment", "exp"), None),
            P(("segment", "exp"), None),
            P("segment", "exp", None, None),
            P("segment", "exp", None, None),
        ),
        check_vma=False,
    )
```

```python
import functools

import jax
import jax.numpy as jnp
from jax import lax
from jax.experimental import pallas as pl
from jax.experimental.pallas import tpu as pltpu
from jax.sharding import PartitionSpec as P


MB_TOK = 64
MATE, FAR, OUTER = 1, 2, 3
SIZES = (24, 16, 16)
RETURNS = ((0, 1), (2,))
F32 = jnp.float32
BF16 = jnp.bfloat16


def swapped(value, mask):
    pairs = [(source, source ^ mask) for source in range(lax.axis_size("segment"))]
    return lax.ppermute(value, "segment", pairs)


def rms_norm(values, gain):
    mean_square = jnp.mean(values * values, axis=-1, keepdims=True)
    return values * lax.rsqrt(mean_square + 1e-06) * gain


def exchanged(value):
    return lax.all_to_all(value, "exp", split_axis=0, concat_axis=0, tiled=True)


def dot(left, right, dims):
    return lax.dot_general(left, right, (dims, ((), ())), preferred_element_type=F32)


def layer(
    hidden_rows,
    norm_gain,
    router_weight,
    expert_ids,
    gate_weight,
    up_weight,
    down_weight,
    latent_gain,
    kv_weight,
):
    columns = lax.axis_size("exp")
    model_width = hidden_rows.shape[1]
    width_half = model_width // 2
    experts = router_weight.shape[1]
    top_count = expert_ids.shape[1]
    rows = hidden_rows.shape[0]
    capacity = MB_TOK * top_count * 5 // (4 * experts)
    segment = lax.axis_index("segment")
    half = segment % 2
    pair = segment // 2
    w_gate = gate_weight[0, 0]
    w_up = up_weight[0, 0]
    w_down = down_weight[0, 0]

    residual = hidden_rows.astype(F32)
    normed = rms_norm(residual, norm_gain).astype(BF16)
    normed, ids_t = lax.optimization_barrier((normed, expert_ids.T))
    ids_mate = swapped(ids_t, MATE)
    rows_mate = swapped(normed, MATE)
    rows_outer = swapped(normed, OUTER)
    ids_outer = swapped(ids_t, OUTER)
    ids_far = swapped(ids_t, FAR)
    mid = rows // 2
    far_low = swapped(rows_outer[:mid], MATE)
    far_high = swapped(rows_mate[mid:], OUTER)
    tokens_pair = jnp.concatenate([normed, rows_mate], axis=0)
    tokens_far = jnp.concatenate([rows_outer, far_low, far_high], axis=0)
    tokens_all = jnp.concatenate([tokens_pair, tokens_far], axis=0)

    own_cols = lax.dynamic_slice_in_dim(w_down, half * width_half, width_half, 1)
    other_cols = lax.dynamic_slice_in_dim(w_down, (1 - half) * width_half, width_half, 1)
    other_cols, far_low, far_high = lax.optimization_barrier((other_cols, far_low, far_high))
    partner_cols = swapped(other_cols, MATE)
    first = half == 0
    down_cols = jnp.concatenate(
        [jnp.where(first, own_cols, partner_cols), jnp.where(first, partner_cols, own_cols)],
        axis=0,
    )

    expert_grid = jnp.arange(experts, dtype=jnp.int32)
    own_grid = expert_grid[:columns] + pair * columns
    block = jnp.arange(rows, dtype=jnp.int32)
    earlier = (block[:, None] < block[None, :]) & (
        block[:, None] // MB_TOK == block[None, :] // MB_TOK
    )
    earlier = earlier.astype(BF16)

    def slots_of(ids, position):
        chosen = jnp.any(ids[:, None, :] == own_grid[None, :, None], axis=0)
        rank = dot(chosen.astype(BF16), earlier, ((1,), (0,))).astype(jnp.int32)
        base = capacity * (block // MB_TOK + position * (rows // MB_TOK))
        return jnp.where(chosen, rank + base[None, :], -1)

    slot_pair = jnp.concatenate([slots_of(ids_t, half), slots_of(ids_mate, 1 - half)], axis=1)
    slot_late, ids_outer, ids_far = lax.optimization_barrier((slot_pair, ids_outer, ids_far))
    slot_far = jnp.concatenate([slots_of(ids_outer, 3 - half), slots_of(ids_far, 2 + half)], axis=1)
    slot_all = jnp.concatenate([slot_late, slot_far], axis=1)
    ids_all = jnp.concatenate([ids_t, ids_mate, ids_outer, ids_far], axis=1)

    def hits(slot, low, size):
        grid = low + jnp.arange(size, dtype=jnp.int32)
        return slot[:, None, :] == grid[None, :, None]

    chosen = jnp.any(ids_all[:, None, :] == expert_grid[None, :, None], axis=0)
    logits_t = dot(router_weight, tokens_all, ((0,), (1,)))
    affinity = jnp.where(chosen, jax.nn.sigmoid(logits_t), 0.0)
    share_all = affinity / jnp.sum(affinity, axis=0, keepdims=True)
    share = lax.dynamic_slice_in_dim(share_all, pair * columns, columns, 0)

    lows = [sum(SIZES[:i]) for i in range(len(SIZES))]
    sides = ((slot_pair, tokens_pair), (slot_all, tokens_all), (slot_far, tokens_far))
    counts = jnp.sum((slot_all >= 0).astype(F32), axis=1)
    last = len(SIZES) - 1
    received = []
    count_total = None
    for index, (low, size) in enumerate(zip(lows, SIZES)):
        slot, tokens = sides[index]
        picks = hits(slot, low, size).astype(BF16).reshape(columns * size, slot.shape[1])
        buffer = dot(picks, tokens, ((1,), (0,))).astype(BF16)
        buffer = buffer.reshape(columns, size, model_width)
        if index == last:
            extra = jnp.broadcast_to(counts.astype(BF16)[:, None, None], (columns, size, 128))
            buffer = jnp.concatenate([buffer, extra], axis=2)
        if index == last:
            arrived = exchanged(buffer)
            count_total = jnp.sum(arrived[:, 0, model_width].astype(F32))
            arrived = arrived[:, :, :model_width]
        else:
            arrived = exchanged(buffer)
        received.append(arrived.reshape(columns * size, model_width))
    hidden, full, outs = [], [], []
    for value in received:
        gate_pre = dot(w_gate, value, ((1,), (1,)))
        up_pre = dot(w_up, value, ((1,), (1,)))
        own_t = (jax.nn.silu(gate_pre) * up_pre).astype(BF16)
        other_t = swapped(own_t, MATE)
        full_t = jnp.concatenate(
            [jnp.where(first, own_t, other_t), jnp.where(first, other_t, own_t)], axis=0
        )
        out = dot(full_t, down_cols, ((0,), (0,))).astype(BF16)
        hidden.append(own_t)
        full.append(full_t)
        outs.append(out.reshape(columns, -1, width_half))

    mixes = []
    for number, (group, slot, part) in enumerate(
        ((RETURNS[0], slot_all, share), (RETURNS[1], slot_far, share[:, 2 * rows :]))
    ):
        low, size = lows[group[0]], sum(SIZES[i] for i in group)
        sent = jnp.concatenate([outs[i] for i in group], axis=1)
        back = exchanged(sent)
        back = back.reshape(columns * size, width_half)
        table = jnp.where(hits(slot, low, size), part[:, None, :], 0.0)
        table = table.reshape(columns * size, slot.shape[1])
        table = table.astype(BF16)
        if number == 0:
            mixes.append(dot(table, back, ((0,), (0,))))
            continue
        mixes.append(dot(table[:, rows:], back, ((0,), (0,))))
        mixes.append(dot(table[:, :rows], back, ((0,), (0,))))
    mix_own = mixes[0][:rows]
    mix_mate = mixes[0][rows : 2 * rows]
    mix_outer = mixes[0][2 * rows : 3 * rows] + mixes[2]
    mix_far = mixes[0][3 * rows :] + mixes[1]
    from_far = swapped(mix_far.astype(BF16), FAR)
    from_outer = swapped(mix_outer.astype(BF16), OUTER)
    from_mate = swapped(mix_mate.astype(BF16), MATE)
    mine = mix_own + from_far.astype(F32)
    others = from_mate.astype(F32) + from_outer.astype(F32)
    expert_mix = jnp.concatenate(
        [jnp.where(first, mine, others), jnp.where(first, others, mine)], axis=1
    ).astype(BF16)
    combined = residual + expert_mix.astype(F32)
    normed_next = rms_norm(combined, latent_gain).astype(BF16)
    latents = jnp.dot(normed_next, kv_weight, preferred_element_type=F32).astype(BF16)

    inverse_count = 2.0 / count_total
    gram_first = hidden_gram(hidden[:1], full[:1])
    gram_hid = hidden_gram(hidden[1:], full[1:], gram_first, inverse_count)
    gram_in = scaled_gram(half, inverse_count, received, width_half)
    return (expert_mix, latents, gram_in[None, None], gram_hid[None, None])


def gram_kernel(half_ref, scale_ref, *refs):
    count = len(SIZES)
    left, right, out_ref, turned = refs[:count], refs[count : 2 * count], refs[-2], refs[-1]
    ends = [0]
    for ref in left:
        ends.append(ends[-1] + ref.shape[0])

    @pl.when(pl.program_id(1) == 0)
    def _():
        for ref, low, high in zip(left, ends, ends[1:]):
            turned[:, low:high] = ref[...].T

    total = None
    for ref, low, high in zip(right, ends, ends[1:]):
        part = dot(turned[:, low:high], ref[...], ((1,), (0,)))
        total = part if total is None else total + part
    out_ref[...] = total * scale_ref[0, 0]


def scaled_gram(half, scale, chunks, out_rows):
    width = chunks[0].shape[1]
    tile, wide = 512, 512
    steps = out_rows // tile
    left = [
        pl.BlockSpec((c.shape[0], tile), lambda i, j, half: (0, half[0] * steps + i)) for c in chunks
    ]
    right = [pl.BlockSpec((c.shape[0], wide), lambda i, j, half: (0, j)) for c in chunks]
    depth = sum(c.shape[0] for c in chunks)
    return pl.pallas_call(
        gram_kernel,
        grid_spec=pltpu.PrefetchScalarGridSpec(
            num_scalar_prefetch=1,
            grid=(steps, width // wide),
            in_specs=[pl.BlockSpec(memory_space=pltpu.SMEM), *left, *right],
            out_specs=pl.BlockSpec((tile, wide), lambda i, j, half: (i, j)),
            scratch_shapes=[pltpu.VMEM((tile, depth), BF16)],
        ),
        out_shape=jax.ShapeDtypeStruct((out_rows, width), F32),
        cost_estimate=pl.CostEstimate(
            flops=2 * depth * out_rows * width,
            transcendentals=0,
            bytes_accessed=4 * out_rows * width + 6 * depth * width,
        ),
    )(half.astype(jnp.int32).reshape(1), scale.reshape(1, 1), *chunks, *chunks)


def hidden_gram_kernel(count, wide, *refs):
    own, full, out_ref = refs[:count], refs[count : 2 * count], refs[-1]
    width = full[0].shape[0]
    steps, step = width // wide, pl.program_id(0)

    def columns(start, size):
        total = None
        for a_ref, b_ref in zip(own, full):
            part = dot(a_ref[...], b_ref[pl.ds(start, size), :], ((1,), (1,)))
            total = part if total is None else total + part
        if len(refs) > 2 * count + 1:
            base_ref, scale_ref = refs[2 * count : 2 * count + 2]
            total = (total + base_ref[:, pl.ds(start, size)]) * scale_ref[0, 0]
        out_ref[:, pl.ds(start, size)] = total

    @pl.when(step < steps)
    def _():
        columns(pl.multiple_of(step * wide, wide), wide)

    @pl.when(step == steps)
    def _():
        columns(steps * wide, width % wide)


def hidden_gram(own, full, base=None, scale=None):
    units, width = own[0].shape[0], full[0].shape[0]
    wide = 256
    depth = sum(v.shape[1] for v in own)

    def whole(shape):
        return pl.BlockSpec(shape, lambda j: (0, 0), pipeline_mode=pl.Buffered(1))

    operands = (*own, *full)
    specs = [whole(v.shape) for v in operands]
    if base is not None:
        operands += (base, scale.reshape(1, 1))
        specs += [whole(base.shape), pl.BlockSpec(memory_space=pltpu.SMEM)]
    return pl.pallas_call(
        functools.partial(hidden_gram_kernel, len(own), wide),
        grid=(width // wide + 1,),
        in_specs=specs,
        out_specs=pl.BlockSpec((units, width), lambda j: (0, 0)),
        out_shape=jax.ShapeDtypeStruct((units, width), F32),
        cost_estimate=pl.CostEstimate(
            flops=2 * depth * units * width,
            transcendentals=0,
            bytes_accessed=4 * units * width + 2 * depth * (units + width),
        ),
    )(*operands)


def solution(mesh):
    return jax.shard_map(
        layer,
        mesh=mesh,
        in_specs=(
            P(("segment", "exp"), None),
            P(),
            P(),
            P(("segment", "exp"), None),
            P("segment", "exp", None, None),
            P("segment", "exp", None, None),
            P("segment", "exp", None, None),
            P(),
            P(),
        ),
        out_specs=(
            P(("segment", "exp"), None),
            P(("segment", "exp"), None),
            P("segment", "exp", None, None),
            P("segment", "exp", None, None),
        ),
        check_vma=False,
    )
```
